32 devices in a mesh: parts: 2 (over y), gy: 8 (over z, x), gz: 2 (over core).
Axes of the slice: x: 2, y: 2, z: 4, core: 2. Of those that a mesh axis runs over, the one named last changes fastest.
Arguments:
- volume: float32 [512, 16, 512], P('parts', 'gy', 'gz'), parts along dimension 0, may hold values from -96 to 96
- sigma_fine: float32 [3], replicated, may hold values from 0.8 to 2
- sigma_coarse: float32 [3], replicated, may hold values from 2.5 to 4
Outputs:
- dog: float32 [256, 8, 256], P('parts', 'gy', 'gz'), parts along dimension 0
The draws below stay inside these ranges and needn't reach their ends.
There are 2 independent parts, one for each index of `parts`. The reference program is written for one: setup_inputs(seed, part) draws one part's arguments, and reference() takes and returns one part's arrays. A program takes and returns all parts, laid end to end along the dimension named above; an argument that names none is the same for every part. Nothing has to cross between parts.
All inputs are finite; a program needn't handle non-finite values.
Results may differ from the reference program's by a relative error of at most 0.0001.
Values sent between devices are 32-bit elements; how exact they have to be, the bound alone decides.
A program may use at most 64 MiB of HBM per device.

```python
import math
import jax
import jax.numpy as jnp
from jax import lax

X = 256
RADIUS = 30
Y = 16
Z = 512


def stripe_waves(key, length, amplitude):
    subkeys = jax.random.split(key, 3)
    shortest = jnp.array([5.8, 7.6, 11.4, 15.2], jnp.float32)
    longest = jnp.array([5.98, 7.95, 11.95, 15.95], jnp.float32)
    periods = shortest + (longest - shortest) * jax.random.uniform(subkeys[0], (4,), jnp.float32)
    phases = jax.random.uniform(subkeys[1], (4,), jnp.float32)
    scales = amplitude * jax.random.uniform(subkeys[2], (4,), jnp.float32, 0.8, 1.0)
    coords = jnp.arange(length).astype(jnp.float32)
    cycles = jnp.mod(coords[:, None] / periods[None, :] + phases[None, :], 1.0)
    return jnp.sum(scales[None, :] * jnp.cos(2.0 * math.pi * cycles), axis=1)


def draw_volume(key, part):
    subkeys = jax.random.split(key, 4)
    speckle = 12.0 * jax.random.truncated_normal(subkeys[0], -3.0, 3.0, (X, Y, Z), jnp.float32)
    amplitude = 5.0
    along_x = stripe_waves(subkeys[1], X, amplitude)
    along_y = stripe_waves(subkeys[2], Y, amplitude)
    along_z = stripe_waves(subkeys[3], Z, amplitude)
    summed = speckle + along_x[:, None, None] + along_y[None, :, None] + along_z[None, None, :]
    return summed.astype(jnp.float32)


def setup_inputs(seed: int = 0, part: int = 0) -> dict:
    streams_of = jax.random.split(jax.random.key(seed), 4)
    part_keys = jax.random.split(jax.random.fold_in(streams_of[3], part), 4)
    volume = draw_volume(jax.random.fold_in(jax.random.fold_in(streams_of[3], part), 71), part)
    sigma_fine = jnp.clip(jnp.exp(jax.random.uniform(streams_of[1], (3,), jnp.float32, math.log(0.8), math.log(2.0))), 0.8, 2.0)
    sigma_coarse = jnp.clip(jnp.exp(jax.random.uniform(streams_of[2], (3,), jnp.float32, math.log(2.5), math.log(4.0))), 2.5, 4.0)
    return {"volume": volume, "sigma_fine": sigma_fine, "sigma_coarse": sigma_coarse}


def pair_taps(sigma_fine, sigma_coarse, axis_number):
    offsets = jnp.arange(-RADIUS, RADIUS + 1).astype(jnp.float32)
    rows = []
    for sigma in (sigma_fine[axis_number], sigma_coarse[axis_number]):
        values = jnp.exp(-offsets * offsets / (2.0 * sigma * sigma))
        rows.append(values / jnp.sum(values))
    return jnp.stack(rows)


def smooth(padded, weights, axis, count, stride):
    total = None
    for offset in range(weights.shape[1]):
        planes = lax.slice_in_dim(padded, offset, offset + count, stride=stride, axis=axis)
        factor = weights[:, offset].reshape((2, 1, 1, 1))
        term = factor * planes
        total = term if total is None else total + term
    return total


def reference(volume, sigma_fine, sigma_coarse):
    weights_x = pair_taps(sigma_fine, sigma_coarse, 0)
    weights_y = pair_taps(sigma_fine, sigma_coarse, 1)
    weights_z = pair_taps(sigma_fine, sigma_coarse, 2)
    x_count, y_count, z_count = volume.shape
    padded = jnp.pad(volume, ((RADIUS, RADIUS), (0, 0), (0, 0)))
    along_x = smooth(padded, weights_x, 0, x_count, 2)
    padded = jnp.pad(along_x, ((0, 0), (0, 0), (0, 0), (RADIUS, RADIUS)))
    along_z = smooth(padded, weights_z, 3, z_count, 2)
    padded = jnp.pad(along_z, ((0, 0), (0, 0), (RADIUS, RADIUS), (0, 0)))
    along_y = smooth(padded, weights_y, 2, y_count, 2)
    return along_y[0] - along_y[1]
```

```python
import functools

import jax
import jax.numpy as jnp
from jax import lax
from jax.experimental import pallas as pl
from jax.experimental.pallas import tpu as pltpu
from jax.sharding import PartitionSpec as P

RADIUS = 30
LANES = 128
SUB = 8
CHUNKS = 4
PAIR = 2
MESH = pl.DeviceIdType.MESH


def dot(a, b):
    return jnp.dot(a, b, precision=lax.Precision.HIGHEST, preferred_element_type=jnp.float32)


def splat(value):
    return jnp.full((1, LANES), value, jnp.float32)


def tap_scale(sigma):
    s = splat(sigma)
    rate = 1.0 / (2.0 * s * s)
    t = (lax.broadcasted_iota(jnp.int32, (1, LANES), 1) - RADIUS).astype(jnp.float32)
    e = jnp.where(jnp.abs(t) <= RADIUS, jnp.exp(-(t * t) * rate), 0.0)
    return rate, 1.0 / jnp.broadcast_to(jnp.sum(e, axis=1, keepdims=True), (1, LANES))


def taps_at(distance, scale):
    rate, norm = scale
    d = distance.astype(jnp.float32)
    return jnp.where(jnp.abs(distance) <= RADIUS, jnp.exp(-(d * d) * rate) * norm, 0.0)


def kernel(
    groups, vol, sf, sc, out, vbuf, hbuf, wx, wz, zs, xsend, xrecv, psend, precv,
    load_sem, halo_sems, x_send_sems, x_recv_sems, p_send_sems, p_recv_sems,
):
    x_count, y_rows, z_count = vol.shape
    x_out, z_out = x_count // 2, z_count // 2
    rows = x_out // CHUNKS
    lines = groups // PAIR
    me = lax.axis_index("gy")
    core = lax.axis_index("gz")
    hi, lo = me // PAIR, me % PAIR
    mate = me + 1 - 2 * lo

    barrier = pltpu.get_barrier_semaphore()

    def hello(device):
        pl.semaphore_signal(barrier, inc=1, device_id=device, device_id_type=MESH)

    hello({"gz": 1 - core})
    hello({"gy": mate})
    for k in range(1, lines):
        hello({"gy": ((hi + k) % lines) * PAIR + lo})

    loads = [
        pltpu.make_async_copy(vol.at[:, y, :], vbuf.at[y], load_sem.at[y]) for y in range(y_rows)
    ]
    for load in loads:
        load.start()
    pl.semaphore_wait(barrier, 1 + 1 + (lines - 1))
    edge = pl.multiple_of((1 - core) * (z_count - LANES), LANES)
    halos = [
        pltpu.make_async_remote_copy(
            src_ref=vol.at[:, y, pl.ds(edge, LANES)],
            dst_ref=hbuf.at[y],
            send_sem=halo_sems.at[0, y],
            recv_sem=halo_sems.at[1, y],
            device_id={"gz": 1 - core},
            device_id_type=MESH,
        )
        for y in range(y_rows)
    ]
    for halo in halos:
        halo.start()

    scales = [[tap_scale(ref[a]) for ref in (sf, sc)] for a in range(3)]
    halo_first = z_count - (z_count + LANES) * core
    for s in range(2):
        i = lax.broadcasted_iota(jnp.int32, (z_count, z_out), 0)
        o = lax.broadcasted_iota(jnp.int32, (z_count, z_out), 1)
        wz[:z_count, s * z_out:(s + 1) * z_out] = taps_at(i - 2 * o, scales[2][s])
        i = lax.broadcasted_iota(jnp.int32, (LANES, z_out), 0) + halo_first
        o = lax.broadcasted_iota(jnp.int32, (LANES, z_out), 1)
        wz[z_count:, s * z_out:(s + 1) * z_out] = taps_at(i - 2 * o, scales[2][s])
        for b in range(x_count // LANES):
            o = lax.broadcasted_iota(jnp.int32, (x_out, LANES), 0)
            i = lax.broadcasted_iota(jnp.int32, (x_out, LANES), 1) + b * LANES
            wx[s, :, b * LANES:(b + 1) * LANES] = taps_at(i - 2 * o, scales[0][s])

    for y in range(y_rows):
        loads[y].wait()
        part = dot(vbuf[y], wz[:z_count, :])
        halos[y].wait_recv()
        part = part + dot(hbuf[y], wz[z_count:, :])
        for s in range(2):
            zs[s, :, y * z_out:(y + 1) * z_out] = part[:, s * z_out:(s + 1) * z_out]

    swaps = []
    for c in range(CHUNKS):
        for s in range(2):
            part = dot(wx[s, c * rows:(c + 1) * rows, :], zs[s])
            for y in range(y_rows):
                xsend[c, s * y_rows + y] = part[:, y * z_out:(y + 1) * z_out].reshape(
                    rows // SUB, SUB, z_out
                )
        swap = pltpu.make_async_remote_copy(
            src_ref=xsend.at[c],
            dst_ref=xrecv.at[c],
            send_sem=x_send_sems.at[c],
            recv_sem=x_recv_sems.at[c],
            device_id={"gy": mate},
            device_id_type=MESH,
        )
        swap.start()
        swaps.append(swap)

    def y_tap(s, row, target):
        d = jnp.full((SUB, LANES), row - 2 * target, jnp.int32)
        return taps_at(d, scales[1][s])[None]

    sign = (1.0, -1.0)
    targets = [((hi + k) % lines) * PAIR + lo for k in range(lines)]
    taps = []
    for target in targets:
        taps.append([
            [sign[s] * y_tap(s, owner * y_rows + y, target) for s in range(2) for y in range(y_rows)]
            for owner in (me, mate)
        ])

    order = list(range(1, lines)) + [0]
    pushes = []
    for c in range(CHUNKS):
        swaps[c].wait_recv()
        for k in order:
            total = None
            for held, row_taps in ((xsend, taps[k][0]), (xrecv, taps[k][1])):
                for j, tap in enumerate(row_taps):
                    term = tap * held[c, j]
                    total = term if total is None else total + term
            psend[c, k] = total
            if k:
                push = pltpu.make_async_remote_copy(
                    src_ref=psend.at[c, k],
                    dst_ref=precv.at[c, k],
                    send_sem=p_send_sems.at[c, k],
                    recv_sem=p_recv_sems.at[c, k],
                    device_id={"gy": targets[k]},
                    device_id_type=MESH,
                )
                push.start()
                pushes.append((c, push))

    for c in range(CHUNKS):
        total = psend[c, 0]
        mine = [push for chunk, push in pushes if chunk == c]
        for k, push in enumerate(mine, start=1):
            push.wait_recv()
            total = total + precv[c, k]
        out[c * (rows // SUB):(c + 1) * (rows // SUB)] = total

    for halo in halos:
        halo.wait_send()
    for swap in swaps:
        swap.wait_send()
    for _, push in pushes:
        push.wait_send()


def solution(mesh):
    groups = mesh.shape["gy"]

    def on_device(volume, sigma_fine, sigma_coarse):
        x_count, y_rows, z_count = volume.shape
        x_out, z_out = x_count // 2, z_count // 2
        lines = groups // PAIR
        tile = (x_out // CHUNKS // SUB, SUB, z_out)
        f32 = jnp.float32
        dma = pltpu.SemaphoreType.DMA
        smem = pl.BlockSpec(memory_space=pltpu.SMEM)
        result = pl.pallas_call(
            functools.partial(kernel, groups),
            out_shape=jax.ShapeDtypeStruct((x_out // SUB, SUB, z_out), f32),
            in_specs=[pl.BlockSpec(memory_space=pl.ANY), smem, smem],
            out_specs=pl.BlockSpec(memory_space=pltpu.VMEM),
            scratch_shapes=[
                pltpu.VMEM((y_rows, x_count, z_count), f32),
                pltpu.VMEM((y_rows, x_count, LANES), f32),
                pltpu.VMEM((2, x_out, x_count), f32),
                pltpu.VMEM((z_count + LANES, 2 * z_out), f32),
                pltpu.VMEM((2, x_count, y_rows * z_out), f32),
                pltpu.VMEM((CHUNKS, 2 * y_rows) + tile, f32),
                pltpu.VMEM((CHUNKS, 2 * y_rows) + tile, f32),
                pltpu.VMEM((CHUNKS, lines) + tile, f32),
                pltpu.VMEM((CHUNKS, lines) + tile, f32),
                dma((y_rows,)),
                dma((2, y_rows)),
                dma((CHUNKS,)),
                dma((CHUNKS,)),
                dma((CHUNKS, lines)),
                dma((CHUNKS, lines)),
            ],
            compiler_params=pltpu.CompilerParams(collective_id=0, has_side_effects=True),
        )(volume, sigma_fine, sigma_coarse)
        return result.reshape(x_out, 1, z_out)

    return jax.shard_map(
        on_device,
        mesh=mesh,
        in_specs=(P("parts", "gy", "gz"), P(), P()),
        out_specs=P("parts", "gy", "gz"),
        check_vma=False,
    )
```

```python
import functools

import jax
import jax.numpy as jnp
from jax import lax
from jax.experimental import pallas as pl
from jax.experimental.pallas import tpu as pltpu
from jax.sharding import PartitionSpec as P

RADIUS = 30
LANES = 128
SUB = 8
CHUNKS = 4
PAIR = 2
MESH = pl.DeviceIdType.MESH


def dot(a, b):
    return jnp.dot(a, b, precision=lax.Precision.HIGHEST, preferred_element_type=jnp.float32)


def splat(value):
    return jnp.full((1, LANES), value, jnp.float32)


def tap_scale(sigma):
    s = splat(sigma)
    rate = 1.0 / (2.0 * s * s)
    t = (lax.broadcasted_iota(jnp.int32, (1, LANES), 1) - RADIUS).astype(jnp.float32)
    e = jnp.where(jnp.abs(t) <= RADIUS, jnp.exp(-(t * t) * rate), 0.0)
    return rate, 1.0 / jnp.broadcast_to(jnp.sum(e, axis=1, keepdims=True), (1, LANES))


def taps_at(distance, scale):
    rate, norm = scale
    d = distance.astype(jnp.float32)
    return jnp.where(jnp.abs(distance) <= RADIUS, jnp.exp(-(d * d) * rate) * norm, 0.0)


def kernel(
    groups, vol, sf, sc, out, vbuf, wx, wz, zs, zh, hsend, hrecv, xsend, xrecv, psend, precv,
    load_sem, halo_sems, x_send_sems, x_recv_sems, p_send_sems, p_recv_sems,
):
    x_count, y_rows, z_count = vol.shape
    x_out, z_out = x_count // 2, z_count // 2
    rows = x_out // CHUNKS
    lines = groups // PAIR
    me = lax.axis_index("gy")
    core = lax.axis_index("gz")
    hi, lo = me // PAIR, me % PAIR
    mate = me + 1 - 2 * lo

    barrier = pltpu.get_barrier_semaphore()

    def hello(device):
        pl.semaphore_signal(barrier, inc=1, device_id=device, device_id_type=MESH)

    hello({"gz": 1 - core})
    hello({"gy": mate})
    for k in range(1, lines):
        hello({"gy": ((hi + k) % lines) * PAIR + lo})

    loads = [
        pltpu.make_async_copy(vol.at[:, y, :], vbuf.at[y], load_sem.at[y]) for y in range(y_rows)
    ]
    for load in loads:
        load.start()

    scales = [[tap_scale(ref[a]) for ref in (sf, sc)] for a in range(3)]
    edge = pl.multiple_of((1 - core) * (z_count - LANES), LANES)
    edge_first = (z_count + LANES) * core - LANES
    for s in range(2):
        i = lax.broadcasted_iota(jnp.int32, (z_count, z_out), 0)
        o = lax.broadcasted_iota(jnp.int32, (z_count, z_out), 1)
        wz[:z_count, s * z_out:(s + 1) * z_out] = taps_at(i - 2 * o, scales[2][s])
        i = lax.broadcasted_iota(jnp.int32, (LANES, z_out), 0) + edge_first
        o = lax.broadcasted_iota(jnp.int32, (LANES, z_out), 1)
        wz[z_count:, s * z_out:(s + 1) * z_out] = taps_at(i - 2 * o, scales[2][s])
        for b in range(x_count // LANES):
            o = lax.broadcasted_iota(jnp.int32, (x_out, LANES), 0)
            i = lax.broadcasted_iota(jnp.int32, (x_out, LANES), 1) + b * LANES
            wx[s, :, b * LANES:(b + 1) * LANES] = taps_at(i - 2 * o, scales[0][s])

    for y in range(y_rows):
        loads[y].wait()
        part = dot(vbuf[y], wz[:z_count, :])
        rim = dot(vbuf[y, :, pl.ds(edge, LANES)], wz[z_count:, :])
        for s in range(2):
            zs[s, :, y * z_out:(y + 1) * z_out] = part[:, s * z_out:(s + 1) * z_out]
            zh[s, :, y * z_out:(y + 1) * z_out] = rim[:, s * z_out:(s + 1) * z_out]

    for s in range(2):
        for source, target in ((zs, xsend), (zh, hsend)):
            part = dot(wx[s], source[s])
            for y in range(y_rows):
                target[:, s * y_rows + y] = part[:, y * z_out:(y + 1) * z_out].reshape(
                    CHUNKS, rows // SUB, SUB, z_out
                )

    pl.semaphore_wait(barrier, 1 + 1 + (lines - 1))
    halos = []
    for c in range(CHUNKS):
        halo = pltpu.make_async_remote_copy(
            src_ref=hsend.at[c],
            dst_ref=hrecv.at[c],
            send_sem=halo_sems.at[0, c],
            recv_sem=halo_sems.at[1, c],
            device_id={"gz": 1 - core},
            device_id_type=MESH,
        )
        halo.start()
        halos.append(halo)

    swaps = []
    for c in range(CHUNKS):
        halos[c].wait_recv()
        xsend[c] = xsend[c] + hrecv[c]
        swap = pltpu.make_async_remote_copy(
            src_ref=xsend.at[c],
            dst_ref=xrecv.at[c],
            send_sem=x_send_sems.at[c],
            recv_sem=x_recv_sems.at[c],
            device_id={"gy": mate},
            device_id_type=MESH,
        )
        swap.start()
        swaps.append(swap)

    def weighted(row_taps, held, c):
        total = None
        for j, tap in enumerate(row_taps):
            term = tap * held[c, j]
            total = term if total is None else total + term
        return total

    def y_tap(s, row, target):
        d = jnp.full((SUB, LANES), row - 2 * target, jnp.int32)
        return taps_at(d, scales[1][s])[None]

    sign = (1.0, -1.0)
    targets = [((hi + k) % lines) * PAIR + lo for k in range(lines)]
    taps = []
    for target in targets:
        taps.append([
            [sign[s] * y_tap(s, owner * y_rows + y, target) for s in range(2) for y in range(y_rows)]
            for owner in (me, mate)
        ])

    order = list(range(1, lines)) + [0]
    pushes = []
    for c in range(CHUNKS):
        for k in order:
            psend[c, k] = weighted(taps[k][0], xsend, c)
    for c in range(CHUNKS):
        swaps[c].wait_recv()
        for k in order:
            psend[c, k] = psend[c, k] + weighted(taps[k][1], xrecv, c)
            if k:
                push = pltpu.make_async_remote_copy(
                    src_ref=psend.at[c, k],
                    dst_ref=precv.at[c, k],
                    send_sem=p_send_sems.at[c, k],
                    recv_sem=p_recv_sems.at[c, k],
                    device_id={"gy": targets[k]},
                    device_id_type=MESH,
                )
                push.start()
                pushes.append((c, push))

    for c in range(CHUNKS):
        total = psend[c, 0]
        mine = [push for chunk, push in pushes if chunk == c]
        for k, push in enumerate(mine, start=1):
            push.wait_recv()
            total = total + precv[c, k]
        out[c * (rows // SUB):(c + 1) * (rows // SUB)] = total

    for halo in halos:
        halo.wait_send()
    for swap in swaps:
        swap.wait_send()
    for _, push in pushes:
        push.wait_send()


def solution(mesh):
    groups = mesh.shape["gy"]

    def on_device(volume, sigma_fine, sigma_coarse):
        x_count, y_rows, z_count = volume.shape
        x_out, z_out = x_count // 2, z_count // 2
        lines = groups // PAIR
        tile = (x_out // CHUNKS // SUB, SUB, z_out)
        f32 = jnp.float32
        dma = pltpu.SemaphoreType.DMA
        smem = pl.BlockSpec(memory_space=pltpu.SMEM)
        result = pl.pallas_call(
            functools.partial(kernel, groups),
            out_shape=jax.ShapeDtypeStruct((x_out // SUB, SUB, z_out), f32),
            in_specs=[pl.BlockSpec(memory_space=pl.ANY), smem, smem],
            out_specs=pl.BlockSpec(memory_space=pltpu.VMEM),
            scratch_shapes=[
                pltpu.VMEM((y_rows, x_count, z_count), f32),
                pltpu.VMEM((2, x_out, x_count), f32),
                pltpu.VMEM((z_count + LANES, 2 * z_out), f32),
                pltpu.VMEM((2, x_count, y_rows * z_out), f32),
                pltpu.VMEM((2, x_count, y_rows * z_out), f32),
                pltpu.VMEM((CHUNKS, 2 * y_rows) + tile, f32),
                pltpu.VMEM((CHUNKS, 2 * y_rows) + tile, f32),
                pltpu.VMEM((CHUNKS, 2 * y_rows) + tile, f32),
                pltpu.VMEM((CHUNKS, 2 * y_rows) + tile, f32),
                pltpu.VMEM((CHUNKS, lines) + tile, f32),
                pltpu.VMEM((CHUNKS, lines) + tile, f32),
                dma((y_rows,)),
                dma((2, CHUNKS)),
                dma((CHUNKS,)),
                dma((CHUNKS,)),
                dma((CHUNKS, lines)),
                dma((CHUNKS, lines)),
            ],
            compiler_params=pltpu.CompilerParams(collective_id=0, has_side_effects=True),
        )(volume, sigma_fine, sigma_coarse)
        return result.reshape(x_out, 1, z_out)

    return jax.shard_map(
        on_device,
        mesh=mesh,
        in_specs=(P("parts", "gy", "gz"), P(), P()),
        out_specs=P("parts", "gy", "gz"),
        check_vma=False,
    )
```

```python
import functools

import jax
import jax.numpy as jnp
from jax import lax
from jax.experimental import pallas as pl
from jax.experimental.pallas import tpu as pltpu
from jax.sharding import PartitionSpec as P

RADIUS = 30
LANES = 128
SUB = 8
CHUNKS = 4
RIM = 16
PAIR = 2
MESH = pl.DeviceIdType.MESH


def halves(value):
    high = value.astype(jnp.bfloat16)
    return high, (value - high.astype(jnp.float32)).astype(jnp.bfloat16)


def dot(a, b, dim):
    def term(p, q):
        return lax.dot_general(p, q, (((1,), (dim,)), ((), ())), preferred_element_type=jnp.float32)

    return term(a[0], b[0]) + (term(a[0], b[1]) + term(a[1], b[0]))


def put(ref, place, value):
    for index, half in enumerate(halves(value)):
        ref[(index,) + place] = half


def splat(value):
    return jnp.full((1, LANES), value, jnp.float32)


def tap_scale(sigma):
    s = splat(sigma)
    rate = 1.0 / (2.0 * s * s)
    t = (lax.broadcasted_iota(jnp.int32, (1, LANES), 1) - RADIUS).astype(jnp.float32)
    e = jnp.where(jnp.abs(t) <= RADIUS, jnp.exp(-(t * t) * rate), 0.0)
    return rate, 1.0 / jnp.broadcast_to(jnp.sum(e, axis=1, keepdims=True), (1, LANES))


def taps_at(distance, scale):
    rate, norm = scale
    d = distance.astype(jnp.float32)
    return jnp.where(jnp.abs(distance) <= RADIUS, jnp.exp(-(d * d) * rate) * norm, 0.0)


def kernel(
    groups, vol, sf, sc, out, vbuf, wx, wz, we, zs, zh, hsend, hrecv, xsend, xrecv, psend, precv, whole,
    load_sem, halo_sems, x_send_sems, x_recv_sems, p_send_sems, p_recv_sems,
):
    x_count, y_rows, z_count = vol.shape
    x_out, z_out = x_count // 2, z_count // 2
    rows = z_out // CHUNKS
    lines = groups // PAIR
    me = lax.axis_index("gy")
    core = lax.axis_index("gz")
    hi, lo = me // PAIR, me % PAIR
    mate = me + 1 - 2 * lo

    barrier = pltpu.get_barrier_semaphore()

    def hello(device):
        pl.semaphore_signal(barrier, inc=1, device_id=device, device_id_type=MESH)

    hello({"gz": 1 - core})
    hello({"gy": mate})
    for k in range(1, lines):
        hello({"gy": ((hi + k) % lines) * PAIR + lo})

    loads = [
        pltpu.make_async_copy(vol.at[:, y, :], vbuf.at[y], load_sem.at[y]) for y in range(y_rows)
    ]
    for load in loads:
        load.start()

    scales = [[tap_scale(ref[a]) for ref in (sf, sc)] for a in range(3)]
    edge = pl.multiple_of((1 - core) * (z_count - LANES), LANES)
    edge_first = (z_count + LANES) * core - LANES
    rim_first = (z_out - RIM) * core
    for s in range(2):
        for b in range(z_count // LANES):
            o = lax.broadcasted_iota(jnp.int32, (z_out, LANES), 0)
            i = lax.broadcasted_iota(jnp.int32, (z_out, LANES), 1) + b * LANES
            place = (slice(s * z_out, (s + 1) * z_out), slice(b * LANES, (b + 1) * LANES))
            put(wz, place, taps_at(i - 2 * o, scales[2][s]))
        o = lax.broadcasted_iota(jnp.int32, (RIM, LANES), 0) + rim_first
        i = lax.broadcasted_iota(jnp.int32, (RIM, LANES), 1) + edge_first
        put(we, (slice(s * RIM, (s + 1) * RIM),), taps_at(i - 2 * o, scales[2][s]))
        i = lax.broadcasted_iota(jnp.int32, (x_count, x_out), 0)
        o = lax.broadcasted_iota(jnp.int32, (x_count, x_out), 1)
        put(wx, (s,), taps_at(i - 2 * o, scales[0][s]))

    for y in range(y_rows):
        loads[y].wait()
        part = dot((wz[0], wz[1]), halves(vbuf[y]), 1)
        rim = dot((we[0], we[1]), halves(vbuf[y, :, pl.ds(edge, LANES)]), 1)
        for s in range(2):
            put(zs, (s, slice(y * z_out, (y + 1) * z_out)), part[s * z_out:(s + 1) * z_out])
            put(zh, (s, slice(y * RIM, (y + 1) * RIM)), rim[s * RIM:(s + 1) * RIM])

    for s in range(2):
        part = dot((zs[0, s], zs[1, s]), (wx[0, s], wx[1, s]), 0)
        rim = dot((zh[0, s], zh[1, s]), (wx[0, s], wx[1, s]), 0)
        for y in range(y_rows):
            xsend[:, s * y_rows + y] = part[y * z_out:(y + 1) * z_out].reshape(
                CHUNKS, rows // SUB, SUB, x_out
            )
            hsend[s * y_rows + y] = rim[y * RIM:(y + 1) * RIM].reshape(RIM // SUB, SUB, x_out)

    pl.semaphore_wait(barrier, 1 + 1 + (lines - 1))
    halo = pltpu.make_async_remote_copy(
        src_ref=hsend,
        dst_ref=hrecv,
        send_sem=halo_sems.at[0],
        recv_sem=halo_sems.at[1],
        device_id={"gz": 1 - core},
        device_id_type=MESH,
    )
    halo.start()

    blocks = [c + (CHUNKS - 1 - 2 * c) * core for c in range(CHUNKS)]
    rim_at = (1 - core) * (rows - RIM) // SUB
    swaps = []
    for c in range(CHUNKS):
        if c == CHUNKS - 1:
            halo.wait_recv()
            for j in range(2 * y_rows):
                place = (blocks[c], j, pl.ds(rim_at, RIM // SUB))
                xsend[place] = xsend[place] + hrecv[j]
        swap = pltpu.make_async_remote_copy(
            src_ref=xsend.at[blocks[c]],
            dst_ref=xrecv.at[c],
            send_sem=x_send_sems.at[c],
            recv_sem=x_recv_sems.at[c],
            device_id={"gy": mate},
            device_id_type=MESH,
        )
        swap.start()
        swaps.append(swap)

    def weighted(row_taps, held, c):
        total = None
        for j, tap in enumerate(row_taps):
            term = tap * held[c, j]
            total = term if total is None else total + term
        return total

    def y_tap(s, row, target):
        d = jnp.full((SUB, LANES), row - 2 * target, jnp.int32)
        return taps_at(d, scales[1][s])[None]

    sign = (1.0, -1.0)
    targets = [((hi + k) % lines) * PAIR + lo for k in range(lines)]
    taps = []
    for target in targets:
        taps.append([
            [sign[s] * y_tap(s, owner * y_rows + y, target) for s in range(2) for y in range(y_rows)]
            for owner in (me, mate)
        ])

    order = list(range(1, lines)) + [0]
    pushes = []
    for c in range(CHUNKS):
        for k in order:
            psend[c, k] = weighted(taps[k][0], xsend, blocks[c])
    for c in range(CHUNKS):
        swaps[c].wait_recv()
        for k in order:
            psend[c, k] = psend[c, k] + weighted(taps[k][1], xrecv, c)
            if k:
                push = pltpu.make_async_remote_copy(
                    src_ref=psend.at[c, k],
                    dst_ref=precv.at[c, k],
                    send_sem=p_send_sems.at[c, k],
                    recv_sem=p_recv_sems.at[c, k],
                    device_id={"gy": targets[k]},
                    device_id_type=MESH,
                )
                push.start()
                pushes.append((c, push))

    for c in range(CHUNKS):
        total = psend[c, 0]
        mine = [push for chunk, push in pushes if chunk == c]
        for k, push in enumerate(mine, start=1):
            push.wait_recv()
            total = total + precv[c, k]
        whole[pl.ds(pl.multiple_of(blocks[c] * rows, rows), rows), :] = total.reshape(rows, x_out)

    out[...] = whole[...].T.reshape(x_out // SUB, SUB, z_out)
    halo.wait_send()
    for swap in swaps:
        swap.wait_send()
    for _, push in pushes:
        push.wait_send()


def solution(mesh):
    groups = mesh.shape["gy"]

    def on_device(volume, sigma_fine, sigma_coarse):
        x_count, y_rows, z_count = volume.shape
        x_out, z_out = x_count // 2, z_count // 2
        lines = groups // PAIR
        tile = (z_out // CHUNKS // SUB, SUB, x_out)
        b16 = jnp.bfloat16
        f32 = jnp.float32
        dma = pltpu.SemaphoreType.DMA
        smem = pl.BlockSpec(memory_space=pltpu.SMEM)
        result = pl.pallas_call(
            functools.partial(kernel, groups),
            out_shape=jax.ShapeDtypeStruct((x_out // SUB, SUB, z_out), f32),
            in_specs=[pl.BlockSpec(memory_space=pl.ANY), smem, smem],
            out_specs=pl.BlockSpec(memory_space=pltpu.VMEM),
            scratch_shapes=[
                pltpu.VMEM((y_rows, x_count, z_count), f32),
                pltpu.VMEM((2, 2, x_count, x_out), b16),
                pltpu.VMEM((2, 2 * z_out, z_count), b16),
                pltpu.VMEM((2, 2 * RIM, LANES), b16),
                pltpu.VMEM((2, 2, y_rows * z_out, x_count), b16),
                pltpu.VMEM((2, 2, y_rows * RIM, x_count), b16),
                pltpu.VMEM((2 * y_rows, RIM // SUB, SUB, x_out), f32),
                pltpu.VMEM((2 * y_rows, RIM // SUB, SUB, x_out), f32),
                pltpu.VMEM((CHUNKS, 2 * y_rows) + tile, f32),
                pltpu.VMEM((CHUNKS, 2 * y_rows) + tile, f32),
                pltpu.VMEM((CHUNKS, lines) + tile, f32),
                pltpu.VMEM((CHUNKS, lines) + tile, f32),
                pltpu.VMEM((z_out, x_out), f32),
                dma((y_rows,)),
                dma((2,)),
                dma((CHUNKS,)),
                dma((CHUNKS,)),
                dma((CHUNKS, lines)),
                dma((CHUNKS, lines)),
            ],
            compiler_params=pltpu.CompilerParams(collective_id=0, has_side_effects=True),
        )(volume, sigma_fine, sigma_coarse)
        return result.reshape(x_out, 1, z_out)

    return jax.shard_map(
        on_device,
        mesh=mesh,
        in_specs=(P("parts", "gy", "gz"), P(), P()),
        out_specs=P("parts", "gy", "gz"),
        check_vma=False,
    )
```
